32 devices in a mesh: dp: 4 (over y, x), expert: 8 (over z, core).
Axes of the slice: x: 2, y: 2, z: 4, core: 2. Of those that a mesh axis runs over, the one named last changes fastest.
Arguments:
- tokens: bfloat16 [4096, 4096], P(('dp', 'expert')), may hold values from -6 to 6
- cotangent: bfloat16 [4096, 4096], P(('dp', 'expert')), may hold values from -3 to 3
- expert_ids: int32 [4096, 8, 2], P(('dp', 'expert')), may hold values from 0 to 15, as said below
- slot_ids: int32 [4096, 8, 2], P(('dp', 'expert')), may hold values from 0 to 127, as said below
- route_probs: bfloat16 [4096, 8, 2], P(('dp', 'expert')), may hold values from 0.099609375 to 1
- weights_in: bfloat16 [16, 2, 1792, 512], P('expert', None, 'dp'), may hold values from -0.25 to 0.25
- weights_out: bfloat16 [16, 1792, 512], P('expert', 'dp'), may hold values from -0.125 to 0.125
Outputs:
- grad_tokens: bfloat16 [4096, 4096], P(('dp', 'expert'))
- grad_probs: float32 [4096, 8, 2], P(('dp', 'expert'))
- grad_in: bfloat16 [16, 2, 1792, 512], P('expert', None, 'dp')
- grad_out: bfloat16 [16, 1792, 512], P('expert', 'dp')
The draws below stay inside these ranges and needn't reach their ends.
Inputs may be any that keep to these rules, and one draw needn't show every extreme that they name: `expert_ids`: each sub-token names 2 different experts. On each device the experts fall into two sets of 8, and the two ids of a sub-token come one from each set. Every expert is named by exactly 128 sub-tokens of every device. `slot_ids`: for each device and expert, the sub-tokens of that device that name the expert carry distinct slot numbers at the matching position.
All inputs are finite; a program needn't handle non-finite values.
Results may differ from the reference program's by a relative error of at most 0.012.
Values may be sent and summed in bfloat16 or wider, within the bound.
A program may use at most 192 MiB of HBM per device.

```python
import jax
import jax.numpy as jnp
from jax import lax

H = 8
DS = 512
D = 4096
FF = 1792
TOP = 2
EXPERTS = 16
TOK_DEV = 128
TOKENS = 4096
CAP = 128
N_DP = 4
N_EXPERT = 8
DEVICES = 32


def route_plan(key):
    sub_count = TOK_DEV * H
    half_count = EXPERTS // 2
    pool_size = half_count * CAP
    forced = jax.random.randint(jax.random.fold_in(key, 7), (), 0, EXPERTS)
    positions = jnp.arange(pool_size, dtype=jnp.int32)

    def one_device(device_index):
        device_key = jax.random.fold_in(jax.random.fold_in(key, 13), device_index)
        shuffled = jax.random.permutation(jax.random.fold_in(device_key, 1), EXPERTS)
        picked = []
        for which_half in range(2):
            members = shuffled[which_half * half_count:(which_half + 1) * half_count]
            owners = members[positions // CAP]
            scores = jax.random.randint(jax.random.fold_in(device_key, 2 + which_half), (pool_size,), 0, 2 ** 19) * pool_size + positions
            scores = jnp.where(owners == forced, scores - 2 ** 19 * pool_size, scores)
            chosen = jnp.argsort(scores)[:sub_count]
            chosen = chosen[jax.random.permutation(jax.random.fold_in(device_key, 4 + which_half), sub_count)]
            picked.append((owners[chosen], chosen % CAP))
        swapped = jax.random.randint(jax.random.fold_in(device_key, 6), (sub_count,), 0, 2)
        first_expert = jnp.where(swapped == 1, picked[1][0], picked[0][0])
        second_expert = jnp.where(swapped == 1, picked[0][0], picked[1][0])
        first_slot = jnp.where(swapped == 1, picked[1][1], picked[0][1])
        second_slot = jnp.where(swapped == 1, picked[0][1], picked[1][1])
        expert_table = jnp.stack([first_expert, second_expert], axis=1)
        slot_table = jnp.stack([first_slot, second_slot], axis=1)
        return (expert_table, slot_table)
    expert_table, slot_table = jax.vmap(one_device)(jnp.arange(DEVICES, dtype=jnp.int32))
    return (expert_table.reshape(TOKENS, H, TOP).astype(jnp.int32), slot_table.reshape(TOKENS, H, TOP).astype(jnp.int32))


def draw_expert_ids(key, part):
    return route_plan(key)[0]


def draw_slot_ids(key, part):
    return route_plan(key)[1]


def shard_levels(rng, shape, split, low, largest):
    def one(dim, blocks):
        heights = jax.random.uniform(jax.random.fold_in(jax.random.fold_in(rng, 6), dim), (blocks,), jnp.float32, low / len(split), largest / len(split))
        return jnp.repeat(jnp.exp(heights), shape[dim] // blocks).reshape((-1,) + (1,) * (len(shape) - dim - 1))

    factor_of = one(*split[0])
    for cut in split[1:]:
        factor_of = factor_of * one(*cut)
    return factor_of


def gaussian(stream_key, shape, deviation, limit, split=(), kind=jnp.bfloat16):
    gain = shard_levels(stream_key, shape, split, -0.22, 0.18) if split else 1.0
    drawn = jax.random.normal(stream_key, shape, jnp.float32) * deviation * gain
    return jnp.minimum(jnp.maximum(drawn, -limit), limit).astype(kind)


def setup_inputs(seed: int = 0) -> dict:
    arg_keys = jax.random.split(jax.random.key(seed), 8)
    return {
        "tokens": gaussian(arg_keys[0], (TOKENS, D), 1.0, 6.0, ((0, 32),)),
        "cotangent": gaussian(arg_keys[1], (TOKENS, D), 0.5, 3.0, ((0, 32),)),
        "expert_ids": draw_expert_ids(jax.random.fold_in(arg_keys[7], 71), 0),
        "slot_ids": draw_slot_ids(jax.random.fold_in(arg_keys[7], 71), 0),
        "route_probs": jnp.clip(0.099609375 + 0.9003906 * jax.random.uniform(arg_keys[4], (TOKENS, H, TOP), jnp.float32) ** shard_levels(arg_keys[4], (TOKENS, H, TOP), ((0, 32),), -0.2, 0.2), 0.099609375, 1.0).astype(jnp.bfloat16),
        "weights_in": gaussian(arg_keys[5], (EXPERTS, 2, FF, DS), DS ** -0.5, 0.25, ((0, 8), (2, 4))),
        "weights_out": gaussian(arg_keys[6], (EXPERTS, FF, DS), FF ** -0.5, 0.125, ((0, 8), (1, 4))),
    }


def contract_last(former, latter):
    return lax.dot_general(former, latter, (((1,), (1,)), ((), ())), preferred_element_type=jnp.float32)


def expert_backward(inputs, cotangent, weighting, gate_up, down_proj):
    gate_pre = contract_last(inputs, gate_up[0])
    up_pre = contract_last(inputs, gate_up[1])
    sigmoids = jax.nn.sigmoid(gate_pre)
    activated = gate_pre * sigmoids
    hidden = (activated * up_pre).astype(jnp.bfloat16)
    output = jnp.dot(hidden, down_proj, preferred_element_type=jnp.float32)
    router_grad = jnp.sum(output * cotangent.astype(jnp.float32), axis=1).astype(jnp.bfloat16)
    scaled = (weighting.astype(jnp.float32)[:, None] * cotangent.astype(jnp.float32)).astype(jnp.bfloat16)
    dhidden = contract_last(scaled, down_proj)
    gate_grad = (dhidden * up_pre * sigmoids * (1.0 + gate_pre * (1.0 - sigmoids))).astype(jnp.bfloat16)
    up_grad = (dhidden * activated).astype(jnp.bfloat16)
    input_grad = jnp.dot(gate_grad, gate_up[0], preferred_element_type=jnp.float32)
    input_grad = (input_grad + jnp.dot(up_grad, gate_up[1], preferred_element_type=jnp.float32)).astype(jnp.bfloat16)
    return input_grad, router_grad, gate_grad, up_grad, hidden, scaled


def group_sum(left_rows, grouped):
    left_wide = left_rows.reshape(N_DP, N_EXPERT * CAP, left_rows.shape[1]).astype(jnp.float32)
    partial_sums = jnp.einsum("qrf,qrd->qfd", left_wide, grouped, precision=lax.Precision.HIGHEST)
    rounded = lax.optimization_barrier(partial_sums.astype(jnp.bfloat16))
    return jnp.sum(rounded.astype(jnp.float32), axis=0)


def reference(tokens, cotangent, expert_ids, slot_ids, route_probs, weights_in, weights_out):
    sub_count = TOKENS * H
    buffer_rows = EXPERTS * DEVICES * CAP
    device_of = (jnp.arange(sub_count, dtype=jnp.int32) // (TOK_DEV * H)).astype(jnp.int32)
    placed = expert_ids.reshape(sub_count, TOP).astype(jnp.int32) * (DEVICES * CAP) + device_of[:, None] * CAP + slot_ids.reshape(sub_count, TOP).astype(jnp.int32)
    flat_place = placed.reshape(-1).astype(jnp.int32)

    def spread(values):
        doubled = jnp.broadcast_to(values[:, None, :], (sub_count, TOP, DS)).reshape(sub_count * TOP, DS)
        filled = jnp.zeros((buffer_rows, DS), values.dtype).at[flat_place].set(doubled)
        return filled.reshape(EXPERTS, DEVICES * CAP, DS)

    input_buffer = spread(tokens.reshape(sub_count, DS))
    cotangent_buffer = spread(cotangent.reshape(sub_count, DS))
    prob_buffer = jnp.zeros((buffer_rows,), route_probs.dtype).at[flat_place].set(route_probs.reshape(-1))
    prob_buffer = prob_buffer.reshape(EXPERTS, DEVICES * CAP)

    def one_expert(packed):
        rows_in, rows_cot, rows_prob, gate_up, down_proj = packed
        input_grad, router_grad, gate_grad, up_grad, hidden, scaled = expert_backward(rows_in, rows_cot, rows_prob, gate_up, down_proj)
        grouped = rows_in.reshape(N_DP, N_EXPERT * CAP, DS).astype(jnp.float32)
        gate_sum = group_sum(gate_grad, grouped)
        up_sum = group_sum(up_grad, grouped)
        down_sum = group_sum(hidden, scaled.reshape(N_DP, N_EXPERT * CAP, DS).astype(jnp.float32))
        pair_sum = jnp.stack([gate_sum, up_sum]).astype(jnp.bfloat16)
        return input_grad, router_grad, pair_sum, down_sum.astype(jnp.bfloat16)

    input_grads, router_grads, grad_in, grad_out = lax.map(one_expert, (input_buffer, cotangent_buffer, prob_buffer, weights_in, weights_out))
    back_rows = input_grads.reshape(buffer_rows, DS)[flat_place].reshape(sub_count, TOP, DS).astype(jnp.float32)
    grad_tokens = jnp.sum(back_rows, axis=1).astype(jnp.bfloat16).reshape(TOKENS, D)
    grad_probs = router_grads.reshape(buffer_rows)[flat_place].reshape(TOKENS, H, TOP).astype(jnp.float32)
    return grad_tokens, grad_probs, grad_in, grad_out
```

```python
import jax
import jax.numpy as jnp
from jax import lax
from jax.experimental import pallas as pl
from jax.experimental.pallas import tpu as pltpu
from jax.sharding import PartitionSpec as P

H = 8
DS = 512


def contract_last(former, latter):
    return lax.dot_general(
        former, latter, (((1,), (1,)), ((), ())), preferred_element_type=jnp.float32
    )


def contract_first(former, latter):
    return lax.dot_general(
        former, latter, (((0,), (0,)), ((), ())), preferred_element_type=jnp.float32
    )


def expert_kernel(x_ref, s_ref, w_ref, dx_ref, router_ref, dw_ref, dx_acc, router_acc):
    step = pl.program_id(0)

    @pl.when(step == 0)
    def _():
        dx_acc[...] = jnp.zeros_like(dx_acc)
        router_acc[...] = jnp.zeros_like(router_acc)

    gate_w = w_ref[:, :DS]
    up_w = w_ref[:, DS : 2 * DS]
    down_w = w_ref[:, 2 * DS :]
    x = x_ref[...]
    s = s_ref[...]
    gate_pre = contract_last(x, gate_w)
    up_pre = contract_last(x, up_w)
    dhidden = contract_last(s, down_w)
    sigmoids = jax.nn.sigmoid(gate_pre)
    activated = gate_pre * sigmoids
    hidden = (activated * up_pre).astype(jnp.bfloat16)
    gate_grad = (dhidden * up_pre * sigmoids * (1.0 + gate_pre * (1.0 - sigmoids))).astype(
        jnp.bfloat16
    )
    up_grad = (dhidden * activated).astype(jnp.bfloat16)
    products = hidden.astype(jnp.float32) * dhidden
    folded = products[:, :128]
    for lane in range(128, products.shape[1], 128):
        folded = folded + products[:, lane : lane + 128]
    router_acc[...] += folded
    dx_acc[...] += jnp.dot(gate_grad, gate_w, preferred_element_type=jnp.float32) + jnp.dot(
        up_grad, up_w, preferred_element_type=jnp.float32
    )
    dw_ref[:, :DS] = contract_first(gate_grad, x).astype(jnp.bfloat16)
    dw_ref[:, DS : 2 * DS] = contract_first(up_grad, x).astype(jnp.bfloat16)
    dw_ref[:, 2 * DS :] = contract_first(hidden, s).astype(jnp.bfloat16)

    @pl.when(step == pl.num_programs(0) - 1)
    def _():
        dx_ref[...] = dx_acc[...].astype(jnp.bfloat16)
        router_ref[...] = router_acc[...]


def expert_backward(rows, weights):
    count = rows.shape[0]
    hidden = weights.shape[0]
    block = 256 if hidden % 256 == 0 else 128
    return pl.pallas_call(
        expert_kernel,
        grid=(hidden // block,),
        in_specs=[
            pl.BlockSpec((count, DS), lambda i: (0, 0)),
            pl.BlockSpec((count, DS), lambda i: (0, 1)),
            pl.BlockSpec((block, 3 * DS), lambda i: (i, 0)),
        ],
        out_specs=[
            pl.BlockSpec((count, DS), lambda i: (0, 0)),
            pl.BlockSpec((count, 128), lambda i: (0, 0)),
            pl.BlockSpec((block, 3 * DS), lambda i: (i, 0)),
        ],
        out_shape=[
            jax.ShapeDtypeStruct((count, DS), jnp.bfloat16),
            jax.ShapeDtypeStruct((count, 128), jnp.float32),
            jax.ShapeDtypeStruct((hidden, 3 * DS), jnp.bfloat16),
        ],
        scratch_shapes=[
            pltpu.VMEM((count, DS), jnp.float32),
            pltpu.VMEM((count, 128), jnp.float32),
        ],
        compiler_params=pltpu.CompilerParams(
            dimension_semantics=("arbitrary",), vmem_limit_bytes=48 * 1024 * 1024
        ),
        cost_estimate=pl.CostEstimate(
            flops=16 * count * hidden * DS,
            bytes_accessed=12 * hidden * DS + 6 * count * DS,
            transcendentals=count * hidden,
        ),
    )(rows, rows, weights)


def flip(values, bit):
    size = lax.axis_size("dp")
    return lax.ppermute(values, "dp", [(i, i ^ (1 << bit)) for i in range(size)])


def cuts(length, parts):
    units = length // 16
    edges = [units * k // parts * 16 for k in range(parts)] + [length]
    return list(zip(edges[:-1], edges[1:]))


def bit_orders():
    bits = max(lax.axis_size("dp").bit_length() - 1, 1)
    base = list(range(lax.axis_size("dp").bit_length() - 1))
    return [base[k:] + base[:k] for k in range(bits)]


def gather_weights(packed):
    orders = bit_orders()
    bufs = [packed[lo:hi] for lo, hi in cuts(packed.shape[0], len(orders))]
    for level in range(len(orders[0])):
        moved = [flip(buf, order[level]) for buf, order in zip(bufs, orders)]
        bufs = [jnp.concatenate(pair, axis=0) for pair in zip(bufs, moved)]
    return jnp.concatenate(bufs, axis=0)


def scatter_grads(grads, local_hidden):
    orders = bit_orders()
    size = lax.axis_size("dp")
    spans = cuts(local_hidden, len(orders))
    accs = [grads[lo * size : hi * size] for lo, hi in spans]
    for level in reversed(range(len(orders[0]))):
        halves = [acc.shape[0] // 2 for acc in accs]
        moved = [
            flip(acc[half:], order[level]) for acc, half, order in zip(accs, halves, orders)
        ]
        accs = [
            (acc[:half].astype(jnp.float32) + got.astype(jnp.float32)).astype(jnp.bfloat16)
            for acc, half, got in zip(accs, halves, moved)
        ]
    return jnp.concatenate(accs, axis=0)


def body(tokens, cotangent, expert_ids, slot_ids, route_probs, weights_in, weights_out):
    peers = lax.axis_size("expert")
    local_count = weights_in.shape[0]
    local_hidden = weights_in.shape[2]
    token_count = tokens.shape[0]
    sub_count = token_count * H
    capacity = sub_count * 2 // (local_count * peers)
    expert_rows = peers * capacity
    chosen = expert_ids.reshape(sub_count, 2)
    placed = (
        chosen % local_count * expert_rows
        + chosen // local_count * capacity
        + slot_ids.reshape(sub_count, 2)
    )
    probs = route_probs.reshape(sub_count, 2)
    x = tokens.reshape(sub_count, DS)
    c = cotangent.reshape(sub_count, DS)

    weights = []
    for pos in range(local_count):
        packed = jnp.concatenate(
            [weights_in[pos, 0], weights_in[pos, 1], weights_out[pos]], axis=1
        )
        if weights:
            packed, weights[-1] = lax.optimization_barrier((packed, weights[-1]))
        weights.append(gather_weights(packed))

    arrived = []
    for pos in range(local_count):
        slots = pos * expert_rows + lax.broadcasted_iota(
            jnp.int32, (expert_rows, sub_count), 0
        )
        first = slots == placed[:, 0][None, :]
        second = slots == placed[:, 1][None, :]
        select = (first | second).astype(jnp.bfloat16)
        weigh = jnp.where(
            first, probs[:, 0][None, :], jnp.where(second, probs[:, 1][None, :], 0)
        ).astype(jnp.bfloat16)
        sent = jnp.concatenate(
            [
                jnp.dot(select, x, preferred_element_type=jnp.float32).astype(jnp.bfloat16),
                jnp.dot(weigh, c, preferred_element_type=jnp.float32).astype(jnp.bfloat16),
            ],
            axis=1,
        ).reshape(peers, capacity, 2 * DS)
        if arrived:
            sent, arrived[-1] = lax.optimization_barrier((sent, arrived[-1]))
        arrived.append(lax.all_to_all(sent, "expert", split_axis=0, concat_axis=0, tiled=True))

    total = jnp.zeros((sub_count, DS), jnp.float32)
    routers = []
    grads = []
    for pos in range(local_count):
        dx, router, dw = expert_backward(
            arrived[pos].reshape(expert_rows, 2 * DS), weights[pos]
        )
        grads.append(scatter_grads(dw, local_hidden))
        routers.append(jnp.sum(router, axis=1))
        back = lax.all_to_all(
            dx.reshape(peers, capacity, DS), "expert", split_axis=0, concat_axis=0, tiled=True
        ).reshape(expert_rows, DS)
        slots = pos * expert_rows + lax.broadcasted_iota(
            jnp.int32, (sub_count, expert_rows), 1
        )
        pick = ((slots == placed[:, 0][:, None]) | (slots == placed[:, 1][:, None])).astype(
            jnp.bfloat16
        )
        total = total + jnp.dot(pick, back, preferred_element_type=jnp.float32)
    grad_tokens = total.astype(jnp.bfloat16).reshape(token_count, H * DS)

    router_back = lax.all_to_all(
        jnp.stack(routers).reshape(local_count, peers, capacity),
        "expert",
        split_axis=1,
        concat_axis=1,
        tiled=True,
    ).reshape(local_count * expert_rows)
    slots = lax.broadcasted_iota(jnp.int32, (sub_count, 2, local_count * expert_rows), 2)
    found = jnp.sum(
        jnp.where(slots == placed[:, :, None], router_back[None, None, :], 0.0), axis=2
    )
    grad_probs = (
        (found / probs.astype(jnp.float32))
        .astype(jnp.bfloat16)
        .astype(jnp.float32)
        .reshape(token_count, H, 2)
    )
    grad_in = jnp.stack([jnp.stack([g[:, :DS], g[:, DS : 2 * DS]]) for g in grads])
    grad_out = jnp.stack([g[:, 2 * DS :] for g in grads])
    return (grad_tokens, grad_probs, grad_in, grad_out)


def solution(mesh):
    return jax.shard_map(
        body,
        mesh=mesh,
        in_specs=(
            P(("dp", "expert"), None),
            P(("dp", "expert"), None),
            P(("dp", "expert"), None, None),
            P(("dp", "expert"), None, None),
            P(("dp", "expert"), None, None),
            P("expert", None, "dp", None),
            P("expert", "dp", None),
        ),
        out_specs=(
            P(("dp", "expert"), None),
            P(("dp", "expert"), None, None),
            P("expert", None, "dp", None),
            P("expert", "dp", None),
        ),
        check_vma=False,
    )
```

```python
import jax
import jax.numpy as jnp
from jax import lax
from jax.experimental import pallas as pl
from jax.experimental.pallas import tpu as pltpu
from jax.sharding import PartitionSpec as P

H = 8
DS = 512


def contract_last(former, latter):
    return lax.dot_general(
        former, latter, (((1,), (1,)), ((), ())), preferred_element_type=jnp.float32
    )


def contract_first(former, latter):
    return lax.dot_general(
        former, latter, (((0,), (0,)), ((), ())), preferred_element_type=jnp.float32
    )


def expert_kernel(x_ref, s_ref, w_ref, dx_ref, router_ref, dw_ref, dx_acc, router_acc):
    step = pl.program_id(0)

    @pl.when(step == 0)
    def _():
        dx_acc[...] = jnp.zeros_like(dx_acc)
        router_acc[...] = jnp.zeros_like(router_acc)

    gate_w = w_ref[:, :DS]
    up_w = w_ref[:, DS : 2 * DS]
    down_w = w_ref[:, 2 * DS :]
    x = x_ref[...]
    s = s_ref[...]
    gate_pre = contract_last(x, gate_w)
    up_pre = contract_last(x, up_w)
    dhidden = contract_last(s, down_w)
    sigmoids = jax.nn.sigmoid(gate_pre)
    activated = gate_pre * sigmoids
    hidden = (activated * up_pre).astype(jnp.bfloat16)
    gate_grad = (dhidden * up_pre * sigmoids * (1.0 + gate_pre * (1.0 - sigmoids))).astype(
        jnp.bfloat16
    )
    up_grad = (dhidden * activated).astype(jnp.bfloat16)
    products = hidden.astype(jnp.float32) * dhidden
    folded = products[:, :128]
    for lane in range(128, products.shape[1], 128):
        folded = folded + products[:, lane : lane + 128]
    router_acc[...] += folded
    dx_acc[...] += jnp.dot(gate_grad, gate_w, preferred_element_type=jnp.float32) + jnp.dot(
        up_grad, up_w, preferred_element_type=jnp.float32
    )
    dw_ref[:, :DS] = contract_first(gate_grad, x).astype(jnp.bfloat16)
    dw_ref[:, DS : 2 * DS] = contract_first(up_grad, x).astype(jnp.bfloat16)
    dw_ref[:, 2 * DS :] = contract_first(hidden, s).astype(jnp.bfloat16)

    @pl.when(step == pl.num_programs(0) - 1)
    def _():
        dx_ref[...] = dx_acc[...].astype(jnp.bfloat16)
        router_ref[...] = router_acc[...]


def expert_backward(rows, weights):
    count = rows.shape[0]
    hidden = weights.shape[0]
    block = 256 if hidden % 256 == 0 else 128
    return pl.pallas_call(
        expert_kernel,
        grid=(hidden // block,),
        in_specs=[
            pl.BlockSpec((count, DS), lambda i: (0, 0)),
            pl.BlockSpec((count, DS), lambda i: (0, 1)),
            pl.BlockSpec((block, 3 * DS), lambda i: (i, 0)),
        ],
        out_specs=[
            pl.BlockSpec((count, DS), lambda i: (0, 0)),
            pl.BlockSpec((count, 128), lambda i: (0, 0)),
            pl.BlockSpec((block, 3 * DS), lambda i: (i, 0)),
        ],
        out_shape=[
            jax.ShapeDtypeStruct((count, DS), jnp.bfloat16),
            jax.ShapeDtypeStruct((count, 128), jnp.float32),
            jax.ShapeDtypeStruct((hidden, 3 * DS), jnp.bfloat16),
        ],
        scratch_shapes=[
            pltpu.VMEM((count, DS), jnp.float32),
            pltpu.VMEM((count, 128), jnp.float32),
        ],
        compiler_params=pltpu.CompilerParams(
            dimension_semantics=("arbitrary",), vmem_limit_bytes=48 * 1024 * 1024
        ),
        cost_estimate=pl.CostEstimate(
            flops=16 * count * hidden * DS,
            bytes_accessed=12 * hidden * DS + 6 * count * DS,
            transcendentals=count * hidden,
        ),
    )(rows, rows, weights)


def flip(values, bit):
    size = lax.axis_size("dp")
    return lax.ppermute(values, "dp", [(i, i ^ (1 << bit)) for i in range(size)])


def cuts(length, parts):
    units = length // 16
    edges = [units * k // parts * 16 for k in range(parts)] + [length]
    return list(zip(edges[:-1], edges[1:]))


def bit_orders():
    bits = max(lax.axis_size("dp").bit_length() - 1, 1)
    base = list(range(lax.axis_size("dp").bit_length() - 1))
    return [base[k:] + base[:k] for k in range(bits)]


def gather_weights(packed):
    orders = bit_orders()
    parts = [packed[:, lo:hi] for lo, hi in cuts(packed.shape[1], len(orders))]
    firsts = [flip(part, order[0]) if order else None for part, order in zip(parts, orders)]
    gathered = []
    for pos in range(packed.shape[0]):
        bufs = [
            part[pos] if first is None else jnp.concatenate([part[pos], first[pos]], axis=0)
            for part, first in zip(parts, firsts)
        ]
        if gathered:
            bufs, gathered[-1] = lax.optimization_barrier((bufs, gathered[-1]))
        for level in range(1, len(orders[0])):
            moved = [flip(buf, order[level]) for buf, order in zip(bufs, orders)]
            bufs = [jnp.concatenate(pair, axis=0) for pair in zip(bufs, moved)]
        gathered.append(jnp.concatenate(bufs, axis=0))
    return gathered


def scatter_grads(grads, local_hidden):
    orders = bit_orders()
    size = lax.axis_size("dp")
    spans = cuts(local_hidden, len(orders))
    accs = [grads[lo * size : hi * size] for lo, hi in spans]
    for level in reversed(range(len(orders[0]))):
        halves = [acc.shape[0] // 2 for acc in accs]
        moved = [
            flip(acc[half:], order[level]) for acc, half, order in zip(accs, halves, orders)
        ]
        accs = [
            (acc[:half].astype(jnp.float32) + got.astype(jnp.float32)).astype(jnp.bfloat16)
            for acc, half, got in zip(accs, halves, moved)
        ]
    return jnp.concatenate(accs, axis=0)


def body(tokens, cotangent, expert_ids, slot_ids, route_probs, weights_in, weights_out):
    peers = lax.axis_size("expert")
    local_count = weights_in.shape[0]
    local_hidden = weights_in.shape[2]
    token_count = tokens.shape[0]
    sub_count = token_count * H
    capacity = sub_count * 2 // (local_count * peers)
    expert_rows = peers * capacity
    chosen = expert_ids.reshape(sub_count, 2)
    placed = (
        chosen % local_count * expert_rows
        + chosen // local_count * capacity
        + slot_ids.reshape(sub_count, 2)
    )
    probs = route_probs.reshape(sub_count, 2)
    x = tokens.reshape(sub_count, DS)
    c = cotangent.reshape(sub_count, DS)

    weights = gather_weights(
        jnp.concatenate([weights_in[:, 0], weights_in[:, 1], weights_out], axis=2)
    )

    arrived = []
    for pos in range(local_count):
        slots = pos * expert_rows + lax.broadcasted_iota(
            jnp.int32, (expert_rows, sub_count), 0
        )
        first = slots == placed[:, 0][None, :]
        second = slots == placed[:, 1][None, :]
        select = (first | second).astype(jnp.bfloat16)
        weigh = jnp.where(
            first, probs[:, 0][None, :], jnp.where(second, probs[:, 1][None, :], 0)
        ).astype(jnp.bfloat16)
        sent = jnp.concatenate(
            [
                jnp.dot(select, x, preferred_element_type=jnp.float32).astype(jnp.bfloat16),
                jnp.dot(weigh, c, preferred_element_type=jnp.float32).astype(jnp.bfloat16),
            ],
            axis=1,
        ).reshape(peers, capacity, 2 * DS)
        if arrived:
            sent, arrived[-1] = lax.optimization_barrier((sent, arrived[-1]))
        arrived.append(lax.all_to_all(sent, "expert", split_axis=0, concat_axis=0, tiled=True))

    total = jnp.zeros((sub_count, DS), jnp.float32)
    routers = []
    grads = []
    for pos in range(local_count):
        dx, router, dw = expert_backward(
            arrived[pos].reshape(expert_rows, 2 * DS), weights[pos]
        )
        grads.append(scatter_grads(dw, local_hidden))
        routers.append(jnp.sum(router, axis=1))
        back = lax.all_to_all(
            dx.reshape(peers, capacity, DS), "expert", split_axis=0, concat_axis=0, tiled=True
        ).reshape(expert_rows, DS)
        slots = pos * expert_rows + lax.broadcasted_iota(
            jnp.int32, (sub_count, expert_rows), 1
        )
        pick = ((slots == placed[:, 0][:, None]) | (slots == placed[:, 1][:, None])).astype(
            jnp.bfloat16
        )
        total = total + jnp.dot(pick, back, preferred_element_type=jnp.float32)
    grad_tokens = total.astype(jnp.bfloat16).reshape(token_count, H * DS)

    router_back = lax.all_to_all(
        jnp.stack(routers).reshape(local_count, peers, capacity),
        "expert",
        split_axis=1,
        concat_axis=1,
        tiled=True,
    ).reshape(local_count * expert_rows)
    slots = lax.broadcasted_iota(jnp.int32, (sub_count, 2, local_count * expert_rows), 2)
    found = jnp.sum(
        jnp.where(slots == placed[:, :, None], router_back[None, None, :], 0.0), axis=2
    )
    grad_probs = (
        (found / probs.astype(jnp.float32))
        .astype(jnp.bfloat16)
        .astype(jnp.float32)
        .reshape(token_count, H, 2)
    )
    grad_in = jnp.stack([jnp.stack([g[:, :DS], g[:, DS : 2 * DS]]) for g in grads])
    grad_out = jnp.stack([g[:, 2 * DS :] for g in grads])
    return (grad_tokens, grad_probs, grad_in, grad_out)


def solution(mesh):
    return jax.shard_map(
        body,
        mesh=mesh,
        in_specs=(
            P(("dp", "expert"), None),
            P(("dp", "expert"), None),
            P(("dp", "expert"), None, None),
            P(("dp", "expert"), None, None),
            P(("dp", "expert"), None, None),
            P("expert", None, "dp", None),
            P("expert", "dp", None),
        ),
        out_specs=(
            P(("dp", "expert"), None),
            P(("dp", "expert"), None, None),
            P("expert", None, "dp", None),
            P("expert", "dp", None),
        ),
        check_vma=False,
    )
```

```python
import jax
import jax.numpy as jnp
from jax import lax
from jax.experimental import pallas as pl
from jax.experimental.pallas import tpu as pltpu
from jax.sharding import PartitionSpec as P

H = 8
DS = 512


def contract_last(former, latter):
    return lax.dot_general(
        former, latter, (((1,), (1,)), ((), ())), preferred_element_type=jnp.float32
    )


def contract_first(former, latter):
    return lax.dot_general(
        former, latter, (((0,), (0,)), ((), ())), preferred_element_type=jnp.float32
    )


def expert_kernel(x_ref, s_ref, w_ref, dx_ref, router_ref, dw_ref, dx_acc, router_acc):
    step = pl.program_id(0)

    @pl.when(step == 0)
    def _():
        dx_acc[...] = jnp.zeros_like(dx_acc)
        router_acc[...] = jnp.zeros_like(router_acc)

    gate_w = w_ref[:, :DS]
    up_w = w_ref[:, DS : 2 * DS]
    down_w = w_ref[:, 2 * DS :]
    x = x_ref[...]
    s = s_ref[...]
    gate_pre = contract_last(x, gate_w)
    up_pre = contract_last(x, up_w)
    dhidden = contract_last(s, down_w)
    sigmoids = jax.nn.sigmoid(gate_pre)
    activated = gate_pre * sigmoids
    hidden = (activated * up_pre).astype(jnp.bfloat16)
    gate_grad = (dhidden * up_pre * sigmoids * (1.0 + gate_pre * (1.0 - sigmoids))).astype(
        jnp.bfloat16
    )
    up_grad = (dhidden * activated).astype(jnp.bfloat16)
    products = hidden.astype(jnp.float32) * dhidden
    folded = products[:, :128]
    for lane in range(128, products.shape[1], 128):
        folded = folded + products[:, lane : lane + 128]
    router_acc[...] += folded
    dx_acc[...] += jnp.dot(gate_grad, gate_w, preferred_element_type=jnp.float32) + jnp.dot(
        up_grad, up_w, preferred_element_type=jnp.float32
    )
    dw_ref[:, :DS] = contract_first(gate_grad, x).astype(jnp.bfloat16)
    dw_ref[:, DS : 2 * DS] = contract_first(up_grad, x).astype(jnp.bfloat16)
    dw_ref[:, 2 * DS :] = contract_first(hidden, s).astype(jnp.bfloat16)

    @pl.when(step == pl.num_programs(0) - 1)
    def _():
        dx_ref[...] = dx_acc[...].astype(jnp.bfloat16)
        router_ref[...] = router_acc[...]


def expert_backward(rows, weights):
    count = rows.shape[0]
    hidden = weights.shape[0]
    block = 256 if hidden % 256 == 0 else 128
    return pl.pallas_call(
        expert_kernel,
        grid=(hidden // block,),
        in_specs=[
            pl.BlockSpec((count, DS), lambda i: (0, 0)),
            pl.BlockSpec((count, DS), lambda i: (0, 1)),
            pl.BlockSpec((block, 3 * DS), lambda i: (i, 0)),
        ],
        out_specs=[
            pl.BlockSpec((count, DS), lambda i: (0, 0)),
            pl.BlockSpec((count, 128), lambda i: (0, 0)),
            pl.BlockSpec((block, 3 * DS), lambda i: (i, 0)),
        ],
        out_shape=[
            jax.ShapeDtypeStruct((count, DS), jnp.bfloat16),
            jax.ShapeDtypeStruct((count, 128), jnp.float32),
            jax.ShapeDtypeStruct((hidden, 3 * DS), jnp.bfloat16),
        ],
        scratch_shapes=[
            pltpu.VMEM((count, DS), jnp.float32),
            pltpu.VMEM((count, 128), jnp.float32),
        ],
        compiler_params=pltpu.CompilerParams(
            dimension_semantics=("arbitrary",), vmem_limit_bytes=48 * 1024 * 1024
        ),
        cost_estimate=pl.CostEstimate(
            flops=16 * count * hidden * DS,
            bytes_accessed=12 * hidden * DS + 6 * count * DS,
            transcendentals=count * hidden,
        ),
    )(rows, rows, weights)


def flip(values, bit):
    size = lax.axis_size("dp")
    return lax.ppermute(values, "dp", [(i, i ^ (1 << bit)) for i in range(size)])


def cuts(length, parts):
    units = length // 16
    edges = [units * k // parts * 16 for k in range(parts)] + [length]
    return list(zip(edges[:-1], edges[1:]))


def bit_orders():
    bits = max(lax.axis_size("dp").bit_length() - 1, 1)
    base = list(range(lax.axis_size("dp").bit_length() - 1))
    return [base[k:] + base[:k] for k in range(bits)]


def gather_weights(packed):
    orders = bit_orders()
    parts = [packed[:, lo:hi] for lo, hi in cuts(packed.shape[1], len(orders))]
    firsts = [flip(part, order[0]) if order else None for part, order in zip(parts, orders)]
    gathered = []
    for pos in range(packed.shape[0]):
        bufs = [
            part[pos] if first is None else jnp.concatenate([part[pos], first[pos]], axis=0)
            for part, first in zip(parts, firsts)
        ]
        if gathered:
            bufs, gathered[-1] = lax.optimization_barrier((bufs, gathered[-1]))
        for level in range(1, len(orders[0])):
            moved = [flip(buf, order[level]) for buf, order in zip(bufs, orders)]
            bufs = [jnp.concatenate(pair, axis=0) for pair in zip(bufs, moved)]
        gathered.append(jnp.concatenate(bufs, axis=0))
    return gathered


def scatter_grads(grads, local_hidden, later=None):
    orders = bit_orders()
    size = lax.axis_size("dp")
    spans = cuts(local_hidden, len(orders))
    accs = [grads[lo * size : hi * size] for lo, hi in spans]
    for level in reversed(range(len(orders[0]))):
        halves = [acc.shape[0] // 2 for acc in accs]
        moved = [
            flip(acc[half:], order[level]) for acc, half, order in zip(accs, halves, orders)
        ]
        if later is not None:
            moved, later = lax.optimization_barrier((moved, later))
        accs = [
            (acc[:half].astype(jnp.float32) + got.astype(jnp.float32)).astype(jnp.bfloat16)
            for acc, half, got in zip(accs, halves, moved)
        ]
    return jnp.concatenate(accs, axis=0), later


def body(tokens, cotangent, expert_ids, slot_ids, route_probs, weights_in, weights_out):
    peers = lax.axis_size("expert")
    local_count = weights_in.shape[0]
    local_hidden = weights_in.shape[2]
    token_count = tokens.shape[0]
    sub_count = token_count * H
    capacity = sub_count * 2 // (local_count * peers)
    expert_rows = peers * capacity
    chosen = expert_ids.reshape(sub_count, 2)
    placed = (
        chosen % local_count * expert_rows
        + chosen // local_count * capacity
        + slot_ids.reshape(sub_count, 2)
    )
    probs = route_probs.reshape(sub_count, 2)
    x = tokens.reshape(sub_count, DS)
    c = cotangent.reshape(sub_count, DS)

    weights = gather_weights(
        jnp.concatenate([weights_in[:, 0], weights_in[:, 1], weights_out], axis=2)
    )

    arrived = []
    for pos in range(local_count):
        slots = pos * expert_rows + lax.broadcasted_iota(
            jnp.int32, (expert_rows, sub_count), 0
        )
        first = slots == placed[:, 0][None, :]
        second = slots == placed[:, 1][None, :]
        select = (first | second).astype(jnp.bfloat16)
        weigh = jnp.where(
            first, probs[:, 0][None, :], jnp.where(second, probs[:, 1][None, :], 0)
        ).astype(jnp.bfloat16)
        sent = jnp.concatenate(
            [
                jnp.dot(select, x, preferred_element_type=jnp.float32).astype(jnp.bfloat16),
                jnp.dot(weigh, c, preferred_element_type=jnp.float32).astype(jnp.bfloat16),
            ],
            axis=1,
        ).reshape(peers, capacity, 2 * DS)
        if arrived:
            sent, arrived[-1] = lax.optimization_barrier((sent, arrived[-1]))
        arrived.append(lax.all_to_all(sent, "expert", split_axis=0, concat_axis=0, tiled=True))

    total = jnp.zeros((sub_count, DS), jnp.float32)
    routers = []
    grads = []
    outs = [
        expert_backward(arrived[pos].reshape(expert_rows, 2 * DS), weights[pos])
        for pos in range(local_count)
    ]
    pending = [out[2] for out in outs]
    for pos in range(local_count):
        dx, router, _ = outs[pos]
        later = pending[pos + 1] if pos + 1 < local_count else None
        scattered, later = scatter_grads(pending[pos], local_hidden, later)
        if later is not None:
            pending[pos + 1] = later
        grads.append(scattered)
        routers.append(jnp.sum(router, axis=1))
        back = lax.all_to_all(
            dx.reshape(peers, capacity, DS), "expert", split_axis=0, concat_axis=0, tiled=True
        ).reshape(expert_rows, DS)
        slots = pos * expert_rows + lax.broadcasted_iota(
            jnp.int32, (sub_count, expert_rows), 1
        )
        pick = ((slots == placed[:, 0][:, None]) | (slots == placed[:, 1][:, None])).astype(
            jnp.bfloat16
        )
        total = total + jnp.dot(pick, back, preferred_element_type=jnp.float32)
    grad_tokens = total.astype(jnp.bfloat16).reshape(token_count, H * DS)

    router_back = lax.all_to_all(
        jnp.stack(routers).reshape(local_count, peers, capacity),
        "expert",
        split_axis=1,
        concat_axis=1,
        tiled=True,
    ).reshape(local_count * expert_rows)
    slots = lax.broadcasted_iota(jnp.int32, (sub_count, 2, local_count * expert_rows), 2)
    found = jnp.sum(
        jnp.where(slots == placed[:, :, None], router_back[None, None, :], 0.0), axis=2
    )
    grad_probs = (
        (found / probs.astype(jnp.float32))
        .astype(jnp.bfloat16)
        .astype(jnp.float32)
        .reshape(token_count, H, 2)
    )
    grad_in = jnp.stack([jnp.stack([g[:, :DS], g[:, DS : 2 * DS]]) for g in grads])
    grad_out = jnp.stack([g[:, 2 * DS :] for g in grads])
    return (grad_tokens, grad_probs, grad_in, grad_out)


def solution(mesh):
    return jax.shard_map(
        body,
        mesh=mesh,
        in_specs=(
            P(("dp", "expert"), None),
            P(("dp", "expert"), None),
            P(("dp", "expert"), None, None),
            P(("dp", "expert"), None, None),
            P(("dp", "expert"), None, None),
            P("expert", None, "dp", None),
            P("expert", "dp", None),
        ),
        out_specs=(
            P(("dp", "expert"), None),
            P(("dp", "expert"), None, None),
            P("expert", None, "dp", None),
            P("expert", "dp", None),
        ),
        check_vma=False,
    )
```
